256 devices in a mesh: dp: 8 (over x, core), ctx: 32 (over y, z).
Axes of the slice: x: 4, y: 4, z: 8, core: 2. Of those that a mesh axis runs over, the one named last changes fastest.
Arguments:
- tile_embed: bfloat16 [8, 32, 512, 1536], P(None, 'ctx', 'dp'), may hold values from -8 to 8
- tile_counts: int32 [8], replicated, may hold values from 4096 to 16384
- w_in: bfloat16 [1536, 768], replicated, may hold values from -1 to 1
- w_qkv: bfloat16 [768, 2304], replicated, may hold values from -1 to 1
- w_out: bfloat16 [768, 768], replicated, may hold values from -0.21875 to 0.21875
Outputs:
- mixed: bfloat16 [8, 16384, 768], P('dp', 'ctx')
The draws below stay inside these ranges and needn't reach their ends.
Inputs may be any that keep to these rules, and one draw needn't show every extreme that they name: The tissue tiles of slide s fill its first tile_counts[s] positions; the rest are padding.
All inputs are finite; a program needn't handle non-finite values.
Results may differ from the reference program's by a relative error of at most 0.017.
Values may be sent and summed in bfloat16 or wider, within the bound.
A program may use at most 128 MiB of HBM per device.

```python
import math
import jax
import jax.numpy as jnp
from jax import lax

D = 768
E = 1536
HEAD_TOTAL = 12
ROWS_DEV = 512
SLIDES = 8
N_CTX = 32


def draw_tile_embed(key, part):
    value_key = jax.random.fold_in(jax.random.fold_in(key, 11), 0)
    drawn = jnp.clip(jax.random.normal(value_key, (SLIDES, N_CTX, ROWS_DEV, E), jnp.float32), -6.0, 6.0)
    return drawn.astype(jnp.bfloat16)


def draw_w_in(key, part):
    weights = jnp.clip(jax.random.normal(jax.random.fold_in(key, 12), (E, D), jnp.float32), -6.0, 6.0) * (1.0 / E ** 0.5)
    return jnp.clip(weights, -1.0, 1.0).astype(jnp.bfloat16)


def draw_w_qkv(key, part):
    weights = jnp.clip(jax.random.normal(jax.random.fold_in(key, 13), (D, 3 * D), jnp.float32), -6.0, 6.0) * (3.0 / D) ** 0.5
    return jnp.clip(weights, -1.0, 1.0).astype(jnp.bfloat16)


def touch_ends(array, own_key, smallest, high):
    shape = array.shape
    spot = [jax.random.randint(jax.random.fold_in(own_key, axis), (), 0, shape[axis]) for axis in range(len(shape))]
    array = array.at[tuple(spot)].set(smallest)
    longest = shape.index(max(shape))
    spot[longest] = (spot[longest] + 1) % shape[longest]
    return array.at[tuple(spot)].set(high)


def gaussian(own_key, dims, scale, most, kind=jnp.bfloat16):
    return jnp.clip(scale * jax.random.normal(own_key, dims, jnp.float32), -most, most).astype(kind)


def setup_inputs(seed: int = 0) -> dict:
    key_of = jax.random.split(jax.random.key(seed), 6)
    return {
        "tile_embed": draw_tile_embed(jax.random.fold_in(key_of[5], 71), 0),
        "tile_counts": touch_ends(jax.random.randint(key_of[1], (SLIDES,), ROWS_DEV * N_CTX // 4, ROWS_DEV * N_CTX + 1), jax.random.fold_in(key_of[1], 1), ROWS_DEV * N_CTX // 4, ROWS_DEV * N_CTX).astype(jnp.int32),
        "w_in": draw_w_in(jax.random.fold_in(key_of[5], 71), 0),
        "w_qkv": draw_w_qkv(jax.random.fold_in(key_of[5], 71), 0),
        "w_out": gaussian(key_of[4], (D, D), D ** -0.5, 0.21875),
    }


epsilon = 1e-05

def normalize(values):
    average = lax.optimization_barrier(jnp.mean(values, axis=-1, keepdims=True))
    centered = values - average
    variance = lax.optimization_barrier(jnp.mean(centered * centered, axis=-1, keepdims=True))
    return (centered * lax.rsqrt(variance + epsilon)).astype(jnp.bfloat16)

def attend_rows(qkv, is_valid):
    length = qkv.shape[0]
    model_features = qkv.shape[1] // 3
    head_width = model_features // HEAD_TOTAL
    queries = qkv[:, :model_features].reshape(length, HEAD_TOTAL, head_width).astype(jnp.float32)
    key_rows = qkv[:, model_features:2 * model_features].reshape(length, HEAD_TOTAL, head_width).astype(jnp.float32)
    values = qkv[:, 2 * model_features:].reshape(length, HEAD_TOTAL, head_width).astype(jnp.float32)
    scores = jnp.einsum('qhd,khd->qhk', queries, key_rows) * (1.0 / math.sqrt(head_width))
    key_mask = is_valid[None, None, :]
    running_max = lax.optimization_barrier(jnp.max(jnp.where(key_mask, scores, -1e+30), axis=-1))
    weights = jnp.where(key_mask, jnp.exp(scores - running_max[..., None]), 0.0)
    denominator = lax.optimization_barrier(jnp.sum(weights, axis=-1))
    weighted = jnp.einsum('qhk,khd->qhd', weights.astype(jnp.bfloat16).astype(jnp.float32), values)
    return (weighted, running_max, denominator)

def reference(tile_embed, tile_counts, w_in, w_qkv, w_out):
    slide_total, context_count, row_count, embed_width = tile_embed.shape
    sequence_length = context_count * row_count
    model_features = w_out.shape[0]
    head_width = model_features // HEAD_TOTAL
    results = []
    for slide_index in range(slide_total):
        embedded = tile_embed[slide_index].reshape(sequence_length, embed_width)
        hidden = jnp.dot(embedded, w_in, preferred_element_type=jnp.float32).astype(jnp.bfloat16)
        normed = normalize(hidden.astype(jnp.float32))
        qkv = jnp.dot(normed, w_qkv, preferred_element_type=jnp.float32).astype(jnp.bfloat16)
        positions = jnp.arange(sequence_length, dtype=jnp.int32)
        is_valid = positions < tile_counts[slide_index]
        local_accumulator, local_maximum, local_total = lax.map(lambda branch_pair: attend_rows(branch_pair[0], branch_pair[1]), (qkv.reshape(context_count, row_count, 3 * model_features), is_valid.reshape(context_count, row_count)))
        local_accumulator = local_accumulator.reshape(sequence_length, HEAD_TOTAL, head_width)
        local_maximum = local_maximum.reshape(sequence_length, HEAD_TOTAL)
        local_total = local_total.reshape(sequence_length, HEAD_TOTAL)
        dilated_branch = qkv.reshape(row_count, context_count, 3 * model_features).transpose(1, 0, 2)
        dilated_validity = is_valid.reshape(row_count, context_count).T
        dilated_accumulator, dilated_maximum, dilated_total = lax.map(lambda branch_pair: attend_rows(branch_pair[0], branch_pair[1]), (dilated_branch, dilated_validity))
        dilated_output = (dilated_accumulator / dilated_total[..., None]).astype(jnp.bfloat16)
        dilated_output = lax.optimization_barrier(dilated_output).astype(jnp.float32)
        dilated_logsumexp = dilated_maximum + jnp.log(dilated_total)
        dilated_output = dilated_output.transpose(1, 0, 2, 3).reshape(sequence_length, HEAD_TOTAL, head_width)
        dilated_logsumexp = dilated_logsumexp.transpose(1, 0, 2).reshape(sequence_length, HEAD_TOTAL)
        combined_output = jnp.maximum(local_maximum, dilated_logsumexp)
        local_weight = jnp.exp(local_maximum - combined_output)
        dilated_weight = jnp.exp(dilated_logsumexp - combined_output)
        attention_fn = (local_weight[..., None] * local_accumulator + dilated_weight[..., None] * dilated_output) / (local_weight * local_total + dilated_weight)[..., None]
        attention_fn = attention_fn.reshape(sequence_length, model_features).astype(jnp.bfloat16)
        mixed = jnp.dot(attention_fn, w_out, preferred_element_type=jnp.float32)
        mixed = jnp.where(is_valid[:, None], mixed, 0.0).astype(jnp.bfloat16)
        results.append(mixed)
    return jnp.stack(results, axis=0)
```

```python
import functools
import math

import jax
import jax.numpy as jnp
from jax import lax
from jax.experimental import pallas as pl
from jax.experimental.pallas import tpu as pltpu
from jax.sharding import PartitionSpec as P

HEAD_TOTAL = 12
HEAD = 64
epsilon = 1e-05
LOG2E = 1.4426950408889634
QB = 256


def project(x, w_ref, valid, q_ref, k_ref, v_ref):
    feat = x.shape[1]
    scale = LOG2E / math.sqrt(HEAD)
    for t in range(feat // 256):
        cols = pl.ds(t * 256, 256)
        q = jnp.dot(x, w_ref[:, pl.ds(t * 256, 256)], preferred_element_type=jnp.float32)
        q_ref[:, cols] = (q * scale).astype(jnp.bfloat16)
        k = jnp.dot(x, w_ref[:, pl.ds(feat + t * 256, 256)], preferred_element_type=jnp.float32)
        k_ref[:, cols] = jnp.where(valid, k, k[0:1, :]).astype(jnp.bfloat16)
        v = jnp.dot(x, w_ref[:, pl.ds(2 * feat + t * 256, 256)], preferred_element_type=jnp.float32)
        v_ref[:, cols] = jnp.where(valid, v, 0.0).astype(jnp.bfloat16)


def attend_pair(q_ref, k_ref, v_ref, ones, pair, rows):
    low = lax.broadcasted_iota(jnp.int32, (1, 128), 1) < HEAD
    cols = pl.ds(pair * 128, 128)
    q = q_ref[rows, cols]
    k = k_ref[:, cols]
    v = jnp.concatenate([v_ref[:, cols], ones], axis=1)
    res = []
    for half in range(2):
        pick = low if half == 0 else jnp.logical_not(low)
        km = jnp.where(pick, k, jnp.zeros_like(k))
        s = lax.dot_general(q, km, (((1,), (1,)), ((), ())), preferred_element_type=jnp.float32)
        m = jnp.max(s, axis=1, keepdims=True)
        p = jnp.exp2(s - m).astype(jnp.bfloat16)
        o = jnp.dot(p, v, preferred_element_type=jnp.float32)
        res.append((o[:, :128], o[:, 128:], m))
    (a0, l0, m0), (a1, l1, m1) = res
    a = jnp.where(low, a0, a1)
    l = jnp.where(low, l0, l1)
    lse0 = m0 + jnp.log2(l0)
    lse1 = m1 + jnp.log2(l1)
    return a / l, lse0, lse1


def attn_kernel(n_ref, x_ref, w_ref, out_ref, lse_ref, q_ref, k_ref, v_ref):
    rows_total = x_ref.shape[0]
    n = n_ref[0]
    row = lax.broadcasted_iota(jnp.int32, (rows_total, 1), 0)
    valid = row < n
    project(x_ref[...], w_ref, valid, q_ref, k_ref, v_ref)
    ones = jnp.where(lax.broadcasted_iota(jnp.int32, (rows_total, 128), 0) < n, 1.0, 0.0).astype(jnp.bfloat16)
    lane = lax.broadcasted_iota(jnp.int32, (1, 128), 1)
    for b in range(rows_total // QB):
        rows = pl.ds(b * QB, QB)
        acc = jnp.zeros((QB, 128), jnp.float32)
        for pair in range(HEAD_TOTAL // 2):
            o, lse0, lse1 = attend_pair(q_ref, k_ref, v_ref, ones, pair, rows)
            out_ref[rows, pl.ds(pair * 128, 128)] = o.astype(out_ref.dtype)
            acc = jnp.where(lane == 2 * pair, lse0, acc)
            acc = jnp.where(lane == 2 * pair + 1, lse1, acc)
        lse_ref[rows, :] = acc


def attention(n, x, w_qkv, out_dtype):
    rows, feat = x.shape
    return pl.pallas_call(
        attn_kernel,
        out_shape=(
            jax.ShapeDtypeStruct((rows, feat), out_dtype),
            jax.ShapeDtypeStruct((rows, 128), jnp.float32),
        ),
        in_specs=[
            pl.BlockSpec(memory_space=pltpu.SMEM),
            pl.BlockSpec(memory_space=pltpu.VMEM),
            pl.BlockSpec(memory_space=pltpu.VMEM),
        ],
        out_specs=(pl.BlockSpec(memory_space=pltpu.VMEM), pl.BlockSpec(memory_space=pltpu.VMEM)),
        scratch_shapes=[pltpu.VMEM((rows, feat), jnp.bfloat16)] * 3,
        cost_estimate=pl.CostEstimate(
            flops=2 * rows * feat * 3 * feat + 4 * rows * rows * feat * 4,
            bytes_accessed=rows * feat * 20,
            transcendentals=rows * rows * HEAD_TOTAL,
        ),
    )(n, x, w_qkv)


def body(tile_embed, tile_counts, w_in, w_qkv, w_out):
    slide_id = lax.axis_index("dp")
    ctx_index = lax.axis_index("ctx")
    context_count = lax.axis_size("ctx")
    slide_total, _, sub_rows, embed_width = tile_embed.shape
    row_count = sub_rows * lax.axis_size("dp")
    feat = w_out.shape[0]
    steps = row_count // context_count
    hidden = jnp.dot(
        tile_embed.reshape(slide_total * sub_rows, embed_width), w_in, preferred_element_type=jnp.float32
    ).astype(jnp.bfloat16).astype(jnp.float32)
    average = jnp.mean(hidden, axis=-1, keepdims=True)
    centered = hidden - average
    variance = jnp.mean(centered * centered, axis=-1, keepdims=True)
    normed = (centered * lax.rsqrt(variance + epsilon)).astype(jnp.bfloat16)
    routed = lax.all_to_all(
        normed.reshape(slide_total, sub_rows, feat), "dp", split_axis=0, concat_axis=0, tiled=True
    ).reshape(row_count, feat)
    tile_number = lax.dynamic_slice_in_dim(tile_counts, slide_id, 1)
    grouped = routed.reshape(steps, context_count, feat).transpose(1, 0, 2)
    dil = lax.all_to_all(grouped, "ctx", split_axis=0, concat_axis=0, tiled=True).reshape(row_count, feat)
    n_local = jnp.clip(tile_number - ctx_index * row_count, 1, row_count)
    n_dil = jnp.clip((tile_number - ctx_index + context_count - 1) // context_count, 1, row_count)
    out_l, lse_l = attention(n_local, routed, w_qkv, jnp.float32)
    out_d, lse_d = attention(n_dil, dil, w_qkv, jnp.bfloat16)
    back = lax.all_to_all(
        out_d.reshape(context_count, steps, feat), "ctx", split_axis=0, concat_axis=0, tiled=True
    )
    back_lse = lax.all_to_all(
        lse_d[:, :16].reshape(context_count, 2, 128), "ctx", split_axis=0, concat_axis=0, tiled=True
    ).reshape(context_count, steps, 16)
    back = back.transpose(1, 0, 2).reshape(row_count, feat).astype(jnp.float32)
    back_lse = back_lse.transpose(1, 0, 2).reshape(row_count, 16)[:, :HEAD_TOTAL]
    share = 1.0 / (1.0 + jnp.exp2(lse_l[:, :HEAD_TOTAL] - back_lse))
    share = jnp.repeat(share, HEAD, axis=1)
    attn = (out_l + share * (back - out_l)).astype(jnp.bfloat16)
    mixed = jnp.dot(attn, w_out, preferred_element_type=jnp.float32)
    positions = ctx_index * row_count + jnp.arange(row_count, dtype=jnp.int32)
    mixed = jnp.where((positions < tile_number[0])[:, None], mixed, 0.0).astype(jnp.bfloat16)
    return mixed.reshape(1, row_count, feat)


def solution(mesh):
    in_specs = (P(None, "ctx", "dp", None), P(), P(), P(), P())
    out_specs = P("dp", "ctx", None)
    return jax.shard_map(body, mesh=mesh, in_specs=in_specs, out_specs=out_specs, check_vma=False)
```
